128 devices in a mesh: sx: 8 (over x, z_hi), sy: 16 (over z_lo, y, core).
Axes of the slice: x: 4, y: 4, z: 4 (z_hi: 2, z_lo: 2; z = z_hi * 2 + z_lo), core: 2. Of those that a mesh axis runs over, the one named last changes fastest.
Arguments:
- interior_rhs: bfloat16 [8, 16, 2048, 1024], P('sx', 'sy'), may hold values from -6 to 6
- interface_coupling: bfloat16 [8, 16, 1024, 2048], P('sx', 'sy'), may hold values from -0.125 to 0.125
- interface_local: float32 [8, 16, 1024, 1024], P('sx', 'sy'), may hold values from -6 to 6
- off_blocks: bfloat16 [8, 16, 16, 4, 128, 128], P('sx', 'sy'), may hold values from -0.125 to 0.125
- diag_inverse: bfloat16 [8, 16, 16, 128, 128], P('sx', 'sy')
- block_pattern: int32 [8, 16, 16, 4], P('sx', 'sy'), may hold values from 0 to 15
- face_order: int32 [8, 16, 2, 512], P('sx', 'sy'), may hold values from 0 to 511, each once within a row
- krylov_map: int32 [8, 16, 1024], P('sx', 'sy'), may hold values from 0 to 1023, each once within a row
Outputs:
- krylov_rows: float32 [8, 16, 1024, 1024], P('sx', 'sy')
The draws below stay inside these ranges and needn't reach their ends.
Inputs may be any that keep to these rules, and one draw needn't show every extreme that they name: Each face_order[i, j, f] is a permutation of 0 to 511. Each krylov_map[i, j] is a permutation of 0 to 1023.
All inputs are finite; a program needn't handle non-finite values.
Results may differ from the reference program's by a relative error of at most 0.0037.
Values sent between devices are 32-bit elements; how exact they have to be, the bound alone decides.
No kernel may reach another device: no remote copies, remote signals or barrier semaphores. Data moves between devices by JAX's collectives and lax.ppermute only.
A program may use at most 128 MiB of HBM per device.

```python
import jax
import jax.numpy as jnp
from jax import lax

BS = 128
FACE = 512
NB = 16
NNZ = 4
SWEEPS = 3
ROWS = 1024
NI = 2048
SHARE = 64
N_SX = 8
N_SY = 16


def draw_diag_inverse(key, part):
    shape = (N_SX, N_SY, NB, BS, BS)
    noise = jax.random.normal(key, shape, jnp.float32)
    eye = jnp.eye(BS, dtype=jnp.float32)
    return (eye + 0.3 * noise / jnp.sqrt(jnp.float32(BS))).astype(jnp.bfloat16)


def touch_ends(values, rng, least, largest):
    spot = [jax.random.randint(jax.random.fold_in(rng, axis), (), 0, length) for axis, length in enumerate(values.shape)]
    main_axis = values.shape.index(max(values.shape))
    next_to = spot[:main_axis] + [(spot[main_axis] + 1) % values.shape[main_axis]] + spot[main_axis + 1:]
    return values.at[tuple(spot)].set(least).at[tuple(next_to)].set(largest)


def level_of(key, shape, split, smallest, top_value):
    def one(dim, blocks):
        draws = jax.random.uniform(jax.random.fold_in(jax.random.fold_in(key, 6), dim), (blocks,), jnp.float32, smallest / len(split), top_value / len(split))
        return jnp.repeat(jnp.exp(draws), shape[dim] // blocks).reshape((-1,) + (1,) * (len(shape) - dim - 1))

    level = one(*split[0])
    for cut in split[1:]:
        level = level * one(*cut)
    return level


def gaussian(own_key, shape, scale, limit, pieces=(), kind=jnp.bfloat16):
    level = level_of(own_key, shape, pieces, -0.22, 0.18) if pieces else 1.0
    drawn = jax.random.normal(own_key, shape, jnp.float32) * scale * level
    return jnp.minimum(jnp.maximum(drawn, -limit), limit).astype(kind)


def setup_inputs(seed: int = 0) -> dict:
    seeds = jax.random.split(jax.random.key(seed), 9)
    return {
        "interior_rhs": gaussian(seeds[0], (N_SX, N_SY, NI, ROWS), 1.0, 6.0, ((0, 8), (1, 16))),
        "interface_coupling": gaussian(seeds[1], (N_SX, N_SY, ROWS, NI), NI ** -0.5, 0.125, ((0, 8), (1, 16))),
        "interface_local": gaussian(seeds[2], (N_SX, N_SY, ROWS, ROWS), 1.0, 6.0, ((0, 8), (1, 16)), jnp.float32),
        "off_blocks": gaussian(seeds[3], (N_SX, N_SY, NB, NNZ, BS, BS), (4 * NNZ * BS) ** -0.5, 0.125, ((0, 8), (1, 16))),
        "diag_inverse": draw_diag_inverse(jax.random.fold_in(seeds[8], 71), 0),
        "block_pattern": touch_ends(jax.random.randint(seeds[5], (N_SX, N_SY, NB, NNZ), 0, NB), jax.random.fold_in(seeds[5], 1), 0, NB - 1).astype(jnp.int32),
        "face_order": jax.vmap(lambda own: jax.random.permutation(own, FACE))(jax.random.split(seeds[6], N_SX * N_SY * 2)).reshape((N_SX, N_SY, 2, FACE)).astype(jnp.int32),
        "krylov_map": jax.vmap(lambda own: jax.random.permutation(own, ROWS))(jax.random.split(seeds[7], N_SX * N_SY)).reshape((N_SX, N_SY, ROWS)).astype(jnp.int32),
    }


def local_schur(rhs, coupling, own, offs, dinv, pattern):
    blocks = rhs.reshape(NB, BS, ROWS)
    dinv_f = dinv.astype(jnp.float32)
    offs_f = offs.astype(jnp.float32)
    z_now = jnp.einsum("bij,bjc->bic", dinv_f, blocks.astype(jnp.float32)).astype(jnp.bfloat16)
    for sweep in range(SWEEPS):
        nearby = z_now[pattern].astype(jnp.float32)
        acc = jnp.einsum("bkij,bkjc->bic", offs_f, nearby)
        resid = (blocks.astype(jnp.float32) - acc).astype(jnp.bfloat16)
        z_now = jnp.einsum("bij,bjc->bic", dinv_f, resid.astype(jnp.float32)).astype(jnp.bfloat16)
    return own - jnp.dot(coupling, z_now.reshape(NI, ROWS), preferred_element_type=jnp.float32)


def reference(interior_rhs, interface_coupling, interface_local, off_blocks, diag_inverse, block_pattern, face_order, krylov_map):
    count = N_SX * N_SY
    flat = (interior_rhs.reshape(count, NI, ROWS), interface_coupling.reshape(count, ROWS, NI),
            interface_local.reshape(count, ROWS, ROWS), off_blocks.reshape(count, NB, NNZ, BS, BS),
            diag_inverse.reshape(count, NB, BS, BS), block_pattern.reshape(count, NB, NNZ))
    schur = lax.map(lambda a: local_schur(*a), flat).reshape(N_SX, N_SY, ROWS, ROWS)
    ordr = face_order
    def shared_of(block, order):
        return block[order][:, order]
    def local_of(block, order):
        inverse = jnp.zeros((FACE,), jnp.int32).at[order].set(jnp.arange(FACE, dtype=jnp.int32))
        return block[inverse][:, inverse]
    face_a = schur[:, :, :FACE, :FACE]
    face_b = schur[:, :, FACE:, FACE:]
    shared_a = jax.vmap(jax.vmap(shared_of))(face_a, ordr[:, :, 0])
    shared_b = jax.vmap(jax.vmap(shared_of))(face_b, ordr[:, :, 1])
    partner_x = jnp.bitwise_xor(jnp.arange(N_SX, dtype=jnp.int32), 1)
    partner_y = jnp.bitwise_xor(jnp.arange(N_SY, dtype=jnp.int32), 1)
    got_a = shared_a[partner_x]
    got_b = shared_b[:, partner_y]
    new_a = face_a + jax.vmap(jax.vmap(local_of))(got_a, ordr[:, :, 0])
    new_b = face_b + jax.vmap(jax.vmap(local_of))(got_b, ordr[:, :, 1])
    top = jnp.concatenate([new_a, schur[:, :, :FACE, FACE:]], axis=3)
    bottom = jnp.concatenate([schur[:, :, FACE:, :FACE], new_b], axis=3)
    assembled = jnp.concatenate([top, bottom], axis=2)
    def place(tile, target):
        return jnp.zeros_like(tile).at[target].set(tile)
    placed = jax.vmap(jax.vmap(place))(assembled, krylov_map)
    placed = placed.reshape(N_SX, N_SY, N_SY, SHARE, ROWS)
    return jnp.transpose(placed, (0, 2, 1, 3, 4)).reshape(N_SX, N_SY, ROWS, ROWS)
```

```python
import functools

import jax
import jax.numpy as jnp
from jax import lax
from jax.experimental import pallas as pl
from jax.experimental.pallas import tpu as pltpu
from jax.sharding import PartitionSpec as P


BS = 128
FACE = 512
NB = 16
NNZ = 4
SWEEPS = 3
ROWS = 1024
NI = 2048
SHARE = 64
OWNERS = ROWS // SHARE
UNROLL = 8
PIECES = 4

f32, bf16 = jnp.float32, jnp.bfloat16
HBM = pl.BlockSpec(memory_space=pltpu.HBM)
VMEM = pl.BlockSpec(memory_space=pltpu.VMEM)
SMEM = pl.BlockSpec(memory_space=pltpu.SMEM)


def swapped(block, axis, bit):
    count = lax.axis_size(axis)
    return lax.ppermute(block, axis, [(low, low ^ 1 << bit) for low in range(count)])


def dot(a, b, dims=((1,), (0,))):
    return lax.dot_general(a, b, (dims, ((), ())), preferred_element_type=f32)


def over_blocks(body, low=0, high=NB, unroll=UNROLL):
    def some(i, carry):
        for u in range(unroll):
            body(low + i * unroll + u)
        return carry

    lax.fori_loop(0, (high - low) // unroll, some, 0)


def rows_of(b):
    return pl.ds(pl.multiple_of(b * BS, BS), BS)


def one_hot_t(order, count):
    width = order.shape[1]
    at = lax.broadcasted_iota(jnp.int32, (count, width), 0)
    return jnp.where(at == order, 1.0, 0.0).astype(bf16)


def schur_kernel(
    face, pattern, order, rhs_hbm, coupling_hbm, own_hbm, offs_hbm, dinv_hbm,
    shared_out, schur_out,
    rhs, coupling, own, offs, dinv, z, resid, sems,
):
    cols = pl.ds(face * FACE, FACE)
    step = NI // PIECES
    blocks = NB // PIECES
    rhs_in = [
        pltpu.make_async_copy(rhs_hbm.at[pl.ds(i * step, step), cols], rhs.at[pl.ds(i * step, step), :], sems.at[i])
        for i in range(PIECES)
    ]
    offs_in = [
        pltpu.make_async_copy(offs_hbm.at[pl.ds(i * blocks, blocks)], offs.at[pl.ds(i * blocks, blocks)], sems.at[PIECES + i])
        for i in range(PIECES)
    ]
    dinv_in = pltpu.make_async_copy(dinv_hbm, dinv, sems.at[2 * PIECES])
    own_in = pltpu.make_async_copy(own_hbm.at[:, cols], own, sems.at[2 * PIECES + 1])
    coupling_in = pltpu.make_async_copy(coupling_hbm, coupling, sems.at[2 * PIECES + 2])
    dinv_in.start()
    for copy in rhs_in + offs_in:
        copy.start()
    coupling_in.start()
    own_in.start()

    def first(b):
        z[rows_of(b), :] = dot(dinv[b], rhs[rows_of(b), :]).astype(bf16)

    dinv_in.wait()
    for i in range(PIECES):
        rhs_in[i].wait()
        over_blocks(first, i * blocks, (i + 1) * blocks, blocks)

    def residual(b):
        row = jnp.concatenate([offs[b, k] for k in range(NNZ)], axis=1)
        near = jnp.concatenate([z[rows_of(pattern[b, k]), :] for k in range(NNZ)], axis=0)
        resid[rows_of(b), :] = (rhs[rows_of(b), :].astype(f32) - dot(row, near)).astype(bf16)

    def relax(b):
        z[rows_of(b), :] = dot(dinv[b], resid[rows_of(b), :]).astype(bf16)

    for copy in offs_in:
        copy.wait()
    for _ in range(SWEEPS):
        over_blocks(residual)
        over_blocks(relax)

    coupling_in.wait()
    own_in.wait()
    for half in (face, 1 - face):
        rows = pl.ds(half * FACE, FACE)
        schur = (own[rows, :] - dot(coupling[rows, :], z[...])).astype(bf16)
        schur_out[rows, :] = schur
        if half == face:
            picker_t = one_hot_t(order[pl.ds(face, 1), :], FACE)
            right = dot(schur, picker_t).astype(bf16)
            shared_out[...] = dot(picker_t, right, ((0,), (0,)))


def schur_half(face, pattern, order, rhs, coupling, own, offs, dinv):
    return pl.pallas_call(
        functools.partial(schur_kernel, face),
        out_shape=(
            jax.ShapeDtypeStruct((FACE, FACE), f32),
            jax.ShapeDtypeStruct((ROWS, FACE), bf16),
        ),
        in_specs=[SMEM, VMEM, HBM, HBM, HBM, HBM, HBM],
        out_specs=(VMEM, VMEM),
        scratch_shapes=[
            pltpu.VMEM((NI, FACE), bf16),
            pltpu.VMEM((ROWS, NI), bf16),
            pltpu.VMEM((ROWS, FACE), f32),
            pltpu.VMEM((NB, NNZ, BS, BS), bf16),
            pltpu.VMEM((NB, BS, BS), bf16),
            pltpu.VMEM((NI, FACE), bf16),
            pltpu.VMEM((NI, FACE), bf16),
            pltpu.SemaphoreType.DMA((2 * PIECES + 3,)),
        ],
        cost_estimate=pl.CostEstimate(flops=9 * 10**9, bytes_accessed=12 * 2**20, transcendentals=0),
        compiler_params=pltpu.CompilerParams(vmem_limit_bytes=32 << 20),
    )(pattern, order, rhs, coupling, own, offs, dinv)


def place_kernel(order, target, left, right, left_out, right_out, left_to, right_to):
    placer = one_hot_t(target[...], ROWS)
    left_out[...] = dot(placer, left[...])
    right_out[...] = dot(placer, right[...])
    for face, out in ((0, left_to), (1, right_to)):
        picker_t = one_hot_t(order[pl.ds(face, 1), :], FACE)
        out[...] = dot(placer[:, face * FACE : (face + 1) * FACE], picker_t).astype(bf16)


def place(order, target, left, right):
    return pl.pallas_call(
        place_kernel,
        name="place",
        out_shape=(
            jax.ShapeDtypeStruct((ROWS, FACE), f32),
            jax.ShapeDtypeStruct((ROWS, FACE), f32),
            jax.ShapeDtypeStruct((ROWS, FACE), bf16),
            jax.ShapeDtypeStruct((ROWS, FACE), bf16),
        ),
        in_specs=[VMEM] * 4,
        out_specs=(VMEM,) * 4,
        cost_estimate=pl.CostEstimate(flops=4 * 10**9, bytes_accessed=8 * 2**20, transcendentals=0),
        compiler_params=pltpu.CompilerParams(vmem_limit_bytes=32 << 20),
    )(order, target, left, right)


def add_kernel(face, order, got, to, own, out_hbm, out, sems):
    picker_t = one_hot_t(order[pl.ds(face, 1), :], FACE)
    local = dot(got[...].astype(bf16), picker_t, ((1,), (1,))).astype(bf16)
    step = ROWS // PIECES
    copies = []
    for i in range(PIECES):
        rows = pl.ds(i * step, step)
        out[rows, :] = own[rows, :] + dot(to[rows, :], local)
        copies.append(pltpu.make_async_copy(out.at[rows, :], out_hbm.at[rows, :], sems.at[i]))
        copies[-1].start()
    for copy in copies:
        copy.wait()


def add_partner(face, order, got, to, own):
    return pl.pallas_call(
        functools.partial(add_kernel, face),
        out_shape=pltpu.HBM((ROWS, FACE), f32),
        in_specs=[VMEM] * 4,
        out_specs=HBM,
        scratch_shapes=[pltpu.VMEM((ROWS, FACE), f32), pltpu.SemaphoreType.DMA((PIECES,))],
        cost_estimate=pl.CostEstimate(flops=10**9, bytes_accessed=6 * 2**20, transcendentals=0),
        compiler_params=pltpu.CompilerParams(vmem_limit_bytes=24 << 20),
    )(order, got, to, own)


def to_owners(placed):
    return lax.all_to_all(placed.reshape(OWNERS, SHARE, FACE), "sy", split_axis=0, concat_axis=0, tiled=True)


def local(
    interior_rhs,
    interface_coupling,
    interface_local,
    off_blocks,
    diag_inverse,
    block_pattern,
    face_order,
    krylov_map,
):
    rhs, coupling, own, offs, dinv = (
        pltpu.with_memory_space_constraint(a[0, 0], pltpu.HBM)
        for a in (interior_rhs, interface_coupling, interface_local, off_blocks, diag_inverse)
    )
    pattern = block_pattern[0, 0]
    order = face_order[0, 0]
    target = krylov_map[0]
    half = functools.partial(
        schur_half, order=order, rhs=rhs, coupling=coupling, own=own, offs=offs, dinv=dinv
    )
    shared_a, left = half(0, pattern)
    got_a = swapped(shared_a, "sx", 0)
    left, pattern = lax.optimization_barrier((left, pattern))
    shared_b, right = half(1, pattern)
    got_b = swapped(shared_b, "sy", 0)
    left_own, right_own, left_to, right_to = place(order, target, left, right)
    right_sum = add_partner(1, order, got_b, right_to, right_own)
    right_all = to_owners(right_sum)
    got_a, right_sum = lax.optimization_barrier((got_a, right_sum))
    left_sum = add_partner(0, order, got_a, left_to, left_own)
    left_all = to_owners(left_sum)
    return jnp.concatenate([left_all, right_all], axis=2).reshape(1, 1, ROWS, ROWS)


def solution(mesh):
    return jax.shard_map(
        local,
        mesh=mesh,
        in_specs=(
            P("sx", "sy", None, None),
            P("sx", "sy", None, None),
            P("sx", "sy", None, None),
            P("sx", "sy", None, None, None, None),
            P("sx", "sy", None, None, None),
            P("sx", "sy", None, None),
            P("sx", "sy", None, None),
            P("sx", "sy", None),
        ),
        out_specs=P("sx", "sy", None, None),
        check_vma=False,
    )
```

```python
import jax
import jax.numpy as jnp
from jax import lax
from jax.experimental import pallas as pl
from jax.experimental.pallas import tpu as pltpu
from jax.sharding import PartitionSpec as P


BS = 128
FACE = 512
NB = 16
NNZ = 4
SWEEPS = 3
ROWS = 1024
NI = 2048
SHARE = 64
OWNERS = ROWS // SHARE
PIECES = 4

f32, bf16 = jnp.float32, jnp.bfloat16
HBM = pl.BlockSpec(memory_space=pltpu.HBM)
VMEM = pl.BlockSpec(memory_space=pltpu.VMEM)
SMEM = pl.BlockSpec(memory_space=pltpu.SMEM)


def swapped(block, axis, bit):
    count = lax.axis_size(axis)
    return lax.ppermute(block, axis, [(low, low ^ 1 << bit) for low in range(count)])


def dot(a, b, dims=((1,), (0,))):
    return lax.dot_general(a, b, (dims, ((), ())), preferred_element_type=f32)


def rows_of(b):
    return pl.ds(b * BS if isinstance(b, int) else pl.multiple_of(b * BS, BS), BS)


def one_hot_t(order, count):
    width = order.shape[1]
    at = lax.broadcasted_iota(jnp.int32, (count, width), 0)
    return jnp.where(at == order, 1.0, 0.0).astype(bf16)


def eliminate(pattern, rhs, offs, dinv, z, resid, small_in, rhs_in, offs_in, dinv_in):
    blocks = NB // PIECES
    dinv_in.wait()
    for i in range(PIECES):
        rhs_in[i].wait()
        for b in range(i * blocks, (i + 1) * blocks):
            z[rows_of(b), :] = dot(dinv[b], rhs[rows_of(b), :]).astype(bf16)
    for copy in (*offs_in, *small_in):
        copy.wait()

    def sweep(_, carry):
        for b in range(NB):
            row = jnp.concatenate([offs[b, k] for k in range(NNZ)], axis=1)
            near = jnp.concatenate([z[rows_of(pattern[k, b]), :] for k in range(NNZ)], axis=0)
            resid[rows_of(b), :] = (rhs[rows_of(b), :].astype(f32) - dot(row, near)).astype(bf16)
        for b in range(NB):
            z[rows_of(b), :] = dot(dinv[b], resid[rows_of(b), :]).astype(bf16)
        return carry

    lax.fori_loop(0, SWEEPS, sweep, 0)


def inputs_in(cols, rhs_hbm, offs_hbm, dinv_hbm, rhs, offs, dinv, sems):
    step = NI // PIECES
    blocks = NB // PIECES
    rhs_in = []
    offs_in = []
    for i in range(PIECES):
        rows, row = pl.ds(i * step, step), pl.ds(i * blocks, blocks)
        rhs_in.append(pltpu.make_async_copy(rhs_hbm.at[rows, cols], rhs.at[rows, :], sems.at[i]))
        offs_in.append(pltpu.make_async_copy(offs_hbm.at[row], offs.at[row], sems.at[PIECES + i]))
    dinv_in = pltpu.make_async_copy(dinv_hbm, dinv, sems.at[2 * PIECES])
    for copy in [dinv_in] + rhs_in + offs_in:
        copy.start()
    return rhs_in, offs_in, dinv_in


def small_inputs_in(pattern_hbm, order_hbm, pattern, order, sems):
    small_in = (
        pltpu.make_async_copy(pattern_hbm, pattern, sems.at[2 * PIECES + 3]),
        pltpu.make_async_copy(order_hbm, order, sems.at[2 * PIECES + 4]),
    )
    for copy in small_in:
        copy.start()
    return small_in


def to_shared(schur, order, face):
    picker_t = one_hot_t(order[pl.ds(face, 1), :], FACE)
    return dot(picker_t, dot(schur, picker_t).astype(bf16), ((0,), (0,)))


def left_kernel(
    pattern_hbm, order_hbm, rhs_hbm, coupling_hbm, own_hbm, offs_hbm, dinv_hbm,
    shared_out, face_out, z_out,
    pattern, order, rhs, coupling, own, offs, dinv, z, resid, face, sems,
):
    cols = pl.ds(0, FACE)
    small_in = small_inputs_in(pattern_hbm, order_hbm, pattern, order, sems)
    waits = inputs_in(cols, rhs_hbm, offs_hbm, dinv_hbm, rhs, offs, dinv, sems)
    own_in = pltpu.make_async_copy(own_hbm.at[cols, cols], own, sems.at[2 * PIECES + 1])
    coupling_in = pltpu.make_async_copy(coupling_hbm.at[cols, :], coupling, sems.at[2 * PIECES + 2])
    coupling_in.start()
    own_in.start()
    eliminate(pattern, rhs, offs, dinv, z, resid, small_in, *waits)
    z_to = pltpu.make_async_copy(z, z_out, sems.at[0])
    z_to.start()
    coupling_in.wait()
    own_in.wait()
    face[...] = (own[...] - dot(coupling[...], z[...])).astype(bf16)
    face_to = pltpu.make_async_copy(face, face_out, sems.at[1])
    face_to.start()
    shared_out[...] = to_shared(face[...], order, 0)
    z_to.wait()
    face_to.wait()


def right_kernel(
    pattern_hbm, order_hbm, rhs_hbm, coupling_hbm, own_hbm, offs_hbm, dinv_hbm,
    shared_out, schur_out,
    pattern, order, rhs, coupling, own, offs, dinv, z, resid, sems,
):
    cols = pl.ds(FACE, FACE)
    small_in = small_inputs_in(pattern_hbm, order_hbm, pattern, order, sems)
    waits = inputs_in(cols, rhs_hbm, offs_hbm, dinv_hbm, rhs, offs, dinv, sems)
    own_in = pltpu.make_async_copy(own_hbm.at[:, cols], own, sems.at[2 * PIECES + 1])
    coupling_in = pltpu.make_async_copy(coupling_hbm, coupling, sems.at[2 * PIECES + 2])
    coupling_in.start()
    own_in.start()
    eliminate(pattern, rhs, offs, dinv, z, resid, small_in, *waits)
    coupling_in.wait()
    own_in.wait()
    for half in (1, 0):
        rows = pl.ds(half * FACE, FACE)
        schur = (own[rows, :] - dot(coupling[rows, :], z[...])).astype(bf16)
        schur_out[rows, :] = schur
        if half == 1:
            shared_out[...] = to_shared(schur, order, 1)


def scratch(rows, *more):
    return [
        pltpu.SMEM((NNZ, NB), jnp.int32),
        pltpu.VMEM((2, FACE), jnp.int32),
        pltpu.VMEM((NI, FACE), bf16),
        pltpu.VMEM((rows, NI), bf16),
        pltpu.VMEM((rows, FACE), f32),
        pltpu.VMEM((NB, NNZ, BS, BS), bf16),
        pltpu.VMEM((NB, BS, BS), bf16),
        pltpu.VMEM((NI, FACE), bf16),
        pltpu.VMEM((NI, FACE), bf16),
        *more,
        pltpu.SemaphoreType.DMA((2 * PIECES + 5,)),
    ]


def left_half(*operands):
    return pl.pallas_call(
        left_kernel,
        name="left_half",
        out_shape=(
            pltpu.VMEM((FACE, FACE), f32),
            pltpu.HBM((FACE, FACE), bf16),
            pltpu.HBM((NI, FACE), bf16),
        ),
        in_specs=[HBM] * 7,
        out_specs=(VMEM, HBM, HBM),
        scratch_shapes=scratch(FACE, pltpu.VMEM((FACE, FACE), bf16)),
        cost_estimate=pl.CostEstimate(flops=5 * 10**9, bytes_accessed=10 * 2**20, transcendentals=0),
        compiler_params=pltpu.CompilerParams(vmem_limit_bytes=20 << 20),
    )(*operands)


def right_half(*operands):
    return pl.pallas_call(
        right_kernel,
        name="right_half",
        out_shape=(
            jax.ShapeDtypeStruct((FACE, FACE), f32),
            jax.ShapeDtypeStruct((ROWS, FACE), bf16),
        ),
        in_specs=[HBM] * 7,
        out_specs=(VMEM,) * 2,
        scratch_shapes=scratch(ROWS),
        cost_estimate=pl.CostEstimate(flops=7 * 10**9, bytes_accessed=12 * 2**20, transcendentals=0),
        compiler_params=pltpu.CompilerParams(vmem_limit_bytes=24 << 20),
    )(*operands)


def place_right_kernel(order, target, right, own_out, to_out):
    placer = one_hot_t(target[...], ROWS)
    own_out[...] = dot(placer, right[...])
    to_out[...] = dot(placer[:, FACE:], one_hot_t(order[pl.ds(1, 1), :], FACE)).astype(bf16)


def place_left_kernel(
    me, order, target, face_hbm, z_hbm, coupling_hbm, own_hbm,
    own_out, to_out,
    face, z, coupling, own, sems,
):
    below = pl.ds(FACE, FACE)
    copies = [
        pltpu.make_async_copy(source, into, sems.at[i])
        for i, (source, into) in enumerate(
            (
                (face_hbm, face),
                (z_hbm, z),
                (coupling_hbm.at[below, :], coupling),
                (own_hbm.at[below, pl.ds(0, FACE)], own),
            )
        )
    ]
    for copy in copies:
        copy.start()
    placer = one_hot_t(target[...] ^ (me[0] * SHARE), ROWS)
    to_out[...] = dot(placer[:, :FACE], one_hot_t(order[pl.ds(0, 1), :], FACE)).astype(bf16)
    copies[0].wait()
    own_out[...] = dot(placer[:, :FACE], face[...])
    for copy in copies[1:]:
        copy.wait()
    rest = (own[...] - dot(coupling[...], z[...])).astype(bf16)
    own_out[...] += dot(placer[:, FACE:], rest)


PLACED = (
    jax.ShapeDtypeStruct((ROWS, FACE), f32),
    jax.ShapeDtypeStruct((ROWS, FACE), bf16),
)


def place_right(*operands):
    return pl.pallas_call(
        place_right_kernel,
        name="place_right",
        out_shape=PLACED,
        in_specs=[VMEM] * 3,
        out_specs=(VMEM,) * 2,
        cost_estimate=pl.CostEstimate(flops=2 * 10**9, bytes_accessed=4 * 2**20, transcendentals=0),
        compiler_params=pltpu.CompilerParams(vmem_limit_bytes=12 << 20),
    )(*operands)


def place_left(*operands):
    return pl.pallas_call(
        place_left_kernel,
        name="place_left",
        out_shape=PLACED,
        in_specs=[SMEM] + [VMEM] * 2 + [HBM] * 4,
        out_specs=(VMEM,) * 2,
        scratch_shapes=[
            pltpu.VMEM((FACE, FACE), bf16),
            pltpu.VMEM((NI, FACE), bf16),
            pltpu.VMEM((FACE, NI), bf16),
            pltpu.VMEM((FACE, FACE), f32),
            pltpu.SemaphoreType.DMA((4,)),
        ],
        cost_estimate=pl.CostEstimate(flops=3 * 10**9, bytes_accessed=8 * 2**20, transcendentals=0),
        compiler_params=pltpu.CompilerParams(vmem_limit_bytes=14 << 20),
    )(*operands)


def from_shared(got, order, face):
    picker_t = one_hot_t(order[pl.ds(face, 1), :], FACE)
    return dot(got[...].astype(bf16), picker_t, ((1,), (1,))).astype(bf16)


def add_right_kernel(order, got, to, own, out_hbm, out, sems):
    local = from_shared(got, order, 1)
    step = ROWS // PIECES
    copies = []
    for i in range(PIECES):
        rows = pl.ds(i * step, step)
        out[rows, :] = own[rows, :] + dot(to[rows, :], local)
        copies.append(pltpu.make_async_copy(out.at[rows, :], out_hbm.at[rows, :], sems.at[i]))
        copies[-1].start()
    for copy in copies:
        copy.wait()


def add_left_kernel(order, got, to, own, *outs):
    local = from_shared(got, order, 0)
    for i, out in enumerate(outs):
        rows = pl.ds(i * SHARE, SHARE)
        out[...] = own[rows, :] + dot(to[rows, :], local)


def add_right(*operands):
    return pl.pallas_call(
        add_right_kernel,
        name="add_right",
        out_shape=pltpu.HBM((ROWS, FACE), f32),
        in_specs=[VMEM] * 4,
        out_specs=HBM,
        scratch_shapes=[pltpu.VMEM((ROWS, FACE), f32), pltpu.SemaphoreType.DMA((PIECES,))],
        cost_estimate=pl.CostEstimate(flops=10**9, bytes_accessed=6 * 2**20, transcendentals=0),
        compiler_params=pltpu.CompilerParams(vmem_limit_bytes=10 << 20),
    )(*operands)


def add_left(*operands):
    return pl.pallas_call(
        add_left_kernel,
        name="add_left",
        out_shape=(jax.ShapeDtypeStruct((SHARE, FACE), f32),) * OWNERS,
        in_specs=[VMEM] * 4,
        out_specs=(VMEM,) * OWNERS,
        cost_estimate=pl.CostEstimate(flops=10**9, bytes_accessed=6 * 2**20, transcendentals=0),
        compiler_params=pltpu.CompilerParams(vmem_limit_bytes=10 << 20),
    )(*operands)


def blank():
    return pl.pallas_call(lambda out: None, name="blank", out_shape=pltpu.HBM((ROWS, ROWS), f32), out_specs=HBM)()


def write_right_kernel(moved, _, out, sem):
    copy = pltpu.make_async_copy(moved, out.at[:, pl.ds(FACE, FACE)], sem)
    copy.start()
    copy.wait()


def write_left_kernel(me, *refs):
    *moved, _, out, sems = refs
    copies = []
    for i, block in enumerate(moved):
        rows = pl.ds(pl.multiple_of((me[0] ^ i) * SHARE, SHARE), SHARE)
        copies.append(pltpu.make_async_copy(block, out.at[rows, pl.ds(0, FACE)], sems.at[i]))
        copies[-1].start()
    for copy in copies:
        copy.wait()


def write(kernel, out, *operands):
    blocks = len(operands)
    return pl.pallas_call(
        kernel,
        out_shape=pltpu.HBM((ROWS, ROWS), f32),
        in_specs=[SMEM if a.shape == (1,) else VMEM for a in operands] + [HBM],
        out_specs=HBM,
        scratch_shapes=[pltpu.SemaphoreType.DMA if blocks == 1 else pltpu.SemaphoreType.DMA((OWNERS,))],
        input_output_aliases={blocks: 0},
        cost_estimate=pl.CostEstimate(flops=0, bytes_accessed=4 * 2**20, transcendentals=0),
        compiler_params=pltpu.CompilerParams(vmem_limit_bytes=4 << 20),
    )(*operands, out)


def to_owners(placed):
    moved = lax.all_to_all(placed.reshape(OWNERS, SHARE, FACE), "sy", split_axis=0, concat_axis=0, tiled=True)
    return moved.reshape(ROWS, FACE)


def to_owner(block, away):
    return lax.ppermute(block, "sy", [(low, low ^ away) for low in range(OWNERS)])


AWAY = (8, 4, 12, 9, 5, 13, 10, 2, 14, 11, 3, 15, 6, 7, 1)


def local(
    interior_rhs,
    interface_coupling,
    interface_local,
    off_blocks,
    diag_inverse,
    block_pattern,
    face_order,
    krylov_map,
):
    rhs, coupling, own, offs, dinv, pattern_in, order_in = (
        pltpu.with_memory_space_constraint(a, pltpu.HBM)
        for a in (
            interior_rhs[0, 0],
            interface_coupling[0, 0],
            interface_local[0, 0],
            off_blocks[0, 0],
            diag_inverse[0, 0],
            block_pattern[0, 0].T,
            face_order[0, 0],
        )
    )
    order = face_order[0, 0]
    target = krylov_map[0]
    me = lax.axis_index("sy").astype(jnp.int32).reshape(1)
    shared_a, face_a, z_left = left_half(pattern_in, order_in, rhs, coupling, own, offs, dinv)
    shared_a, dinv = lax.optimization_barrier((shared_a, dinv))
    dinv = pltpu.with_memory_space_constraint(dinv, pltpu.HBM)
    got_a = swapped(shared_a, "sx", 0)
    shared_b, right = right_half(pattern_in, order_in, rhs, coupling, own, offs, dinv)
    got_b = swapped(shared_b, "sy", 0)
    right_own, right_to = place_right(order, target, right)
    right_sum = add_right(order, got_b, right_to, right_own)
    right_all = to_owners(right_sum)
    z_left, right_sum = lax.optimization_barrier((z_left, right_sum))
    face_a, z_left = (pltpu.with_memory_space_constraint(a, pltpu.HBM) for a in (face_a, z_left))
    left_own, left_to = place_left(me, order, target, face_a, z_left, coupling, own)
    left_sum = add_left(order, got_a, left_to, left_own)
    left_all = list(left_sum)
    for away in AWAY:
        left_all[away] = to_owner(left_sum[away], away)
    out = blank()
    out = write(write_right_kernel, out, right_all)
    out = write(write_left_kernel, out, me, *left_all)
    return out.reshape(1, 1, ROWS, ROWS)


def solution(mesh):
    return jax.shard_map(
        local,
        mesh=mesh,
        in_specs=(
            P("sx", "sy", None, None),
            P("sx", "sy", None, None),
            P("sx", "sy", None, None),
            P("sx", "sy", None, None, None, None),
            P("sx", "sy", None, None, None),
            P("sx", "sy", None, None),
            P("sx", "sy", None, None),
            P("sx", "sy", None),
        ),
        out_specs=P("sx", "sy", None, None),
        check_vma=False,
    )
```
